32 devices in a mesh: dp: 8 (over y, x, core), tensor: 4 (over z).
Axes of the slice: x: 2, y: 2, z: 4, core: 2. Of those that a mesh axis runs over, the one named last changes fastest.
Arguments:
- hidden: bfloat16 [8192, 2048], P(('dp', 'tensor')), may hold values from -6 to 6
- seq_lengths: int32 [8], P('dp'), may hold values from 1 to 1024, 6144 in all
- attn_norm_gain: float32 [2048], P(('dp', 'tensor')), may hold values from 0.5 to 1.5
- attn_norm_bias: float32 [2048], P(('dp', 'tensor')), may hold values from -1.25 to 1.25
- query_weight: bfloat16 [2048, 2048], P('dp', 'tensor'), may hold values from -0.1875 to 0.1875
- key_weight: bfloat16 [2048, 2048], P('dp', 'tensor'), may hold values from -0.1875 to 0.1875
- value_weight: bfloat16 [2048, 2048], P('dp', 'tensor'), may hold values from -0.125 to 0.125
- query_bias: bfloat16 [16, 128], P('tensor', 'dp'), may hold values from -1.25 to 1.25
- value_bias: bfloat16 [16, 128], P('tensor', 'dp'), may hold values from -1.25 to 1.25
- output_weight: bfloat16 [2048, 2048], P('tensor', 'dp'), may hold values from -0.375 to 0.375
- output_bias: float32 [2048], P(('dp', 'tensor')), may hold values from -1.25 to 1.25
- mlp_norm_gain: float32 [2048], P(('dp', 'tensor')), may hold values from 0.5 to 1.5
- mlp_norm_bias: float32 [2048], P(('dp', 'tensor')), may hold values from -1.25 to 1.25
- up_weight: bfloat16 [2048, 8192], P('dp', 'tensor'), may hold values from -0.125 to 0.125
- up_bias: bfloat16 [64, 128], P('tensor', 'dp'), may hold values from -1.25 to 1.25
- down_weight: bfloat16 [8192, 2048], P('tensor', 'dp'), may hold values from -0.09375 to 0.09375
- down_bias: float32 [2048], P(('dp', 'tensor')), may hold values from -1.25 to 1.25
- out_grad: bfloat16 [8192, 2048], P(('dp', 'tensor')), may hold values from -6 to 6
Outputs:
- layer_out: bfloat16 [8192, 2048], P(('dp', 'tensor'))
- hidden_grad: float32 [8192, 2048], P(('dp', 'tensor'))
- attn_norm_gain_grad: float32 [2048], P(('dp', 'tensor'))
- attn_norm_bias_grad: float32 [2048], P(('dp', 'tensor'))
- query_weight_grad: float32 [2048, 2048], P('dp', 'tensor')
- key_weight_grad: float32 [2048, 2048], P('dp', 'tensor')
- value_weight_grad: float32 [2048, 2048], P('dp', 'tensor')
- query_bias_grad: float32 [16, 128], P('tensor', 'dp')
- value_bias_grad: float32 [16, 128], P('tensor', 'dp')
- output_weight_grad: float32 [2048, 2048], P('tensor', 'dp')
- output_bias_grad: float32 [2048], P(('dp', 'tensor'))
- mlp_norm_gain_grad: float32 [2048], P(('dp', 'tensor'))
- mlp_norm_bias_grad: float32 [2048], P(('dp', 'tensor'))
- up_weight_grad: float32 [2048, 8192], P('dp', 'tensor')
- up_bias_grad: float32 [64, 128], P('tensor', 'dp')
- down_weight_grad: float32 [8192, 2048], P('tensor', 'dp')
- down_bias_grad: float32 [2048], P(('dp', 'tensor'))
The draws below stay inside these ranges and needn't reach their ends.
Inputs may be any that keep to these rules, and one draw needn't show every extreme that they name: `seq_lengths`: the number of tokens at the start of each sequence's 1024 slots; the rest are padding.
All inputs are finite; a program needn't handle non-finite values. No bound on the sum of `seq_lengths` on one device may be relied on, other than what follows from the above.
Results may differ from the reference program's by a relative error of at most 0.017.
Values may be sent and summed in bfloat16 or wider, within the bound.
A program may use at most 152 MiB of HBM per device.

```python
import math
import jax
import jax.numpy as jnp
import numpy as np
from jax import lax

D = 2048
H = 16
HD = 128
FF = 8192
LEN = 1024
NSEQ = 8
TOKENS = 8192
N_DP = 8


def shard_levels(rng, shape, cuts, least, top_value):
    gain = 1.0
    for dim, shards_of in cuts:
        heights = jax.random.uniform(jax.random.fold_in(jax.random.fold_in(rng, 6), dim), (shards_of,), jnp.float32, least / len(cuts), top_value / len(cuts))
        gain = gain * jnp.repeat(jnp.exp(heights), shape[dim] // shards_of).reshape((-1,) + (1,) * (len(shape) - 1 - dim))
    return gain


def split_up(number_of, total, most, skew):
    weights = [(1 << 20) // math.isqrt(rank ** skew) + 1 for rank in range(2, number_of + 1)]
    rest, counts = total - most - (number_of - 1), [1] * (number_of - 1)
    while rest > 0:
        free = [i for i in range(number_of - 1) if counts[i] < most]
        mass, remaining = sum([weights[i] for i in free]), rest
        for i in free:
            extra = min(most - counts[i], max(1, remaining * weights[i] // mass), rest)
            counts[i] = counts[i] + extra
            rest = rest - extra
    return np.array([most] + counts)


def ragged(key, amount, total, reach, lean):
    if amount == 2:
        one = jax.random.randint(key, (), max(1, total - reach), min(reach, total - 1) + 1)
        return jnp.stack([one, total - one])
    tallies = jnp.asarray(split_up(amount, total, reach, lean), jnp.int32)
    couples = (amount - 1) // 2
    source_of, taker = tallies[1:1 + 2 * couples:2], tallies[2:2 + 2 * couples:2]
    room = jnp.minimum(source_of - 1, reach - taker)
    shifted = jax.random.randint(jax.random.fold_in(key, 1), (couples,), 0, 1 << 20) % (room + 1)
    tallies = tallies.at[1:1 + 2 * couples:2].set(source_of - shifted).at[2:2 + 2 * couples:2].set(taker + shifted)
    return tallies[jax.random.permutation(jax.random.fold_in(key, 2), amount)]


def scatter_about(stream_key, extent, width, reach, cuts=(), kind=jnp.bfloat16):
    loudness = shard_levels(stream_key, extent, cuts, -0.22, 0.18) if cuts else 1.0
    entries = jax.random.normal(stream_key, extent, jnp.float32) * width * loudness
    return jnp.minimum(jnp.maximum(entries, -reach), reach).astype(kind)


def setup_inputs(seed: int = 0) -> dict:
    streams_of = jax.random.split(jax.random.key(seed), 19)
    hidden = scatter_about(streams_of[0], (TOKENS, D), 1.0, 6.0, ((0, 32),))
    seq_lengths = ragged(streams_of[1], NSEQ, N_DP * LEN * 3 // 4, LEN, 2).astype(jnp.int32)
    attn_norm_gain = jnp.clip(1.0 + 0.1 * jax.random.normal(streams_of[2], (D,), jnp.float32), 0.5, 1.5)
    attn_norm_bias = scatter_about(streams_of[3], (D,), 0.2, 1.25, ((0, 32),), jnp.float32)
    query_weight = scatter_about(streams_of[4], (D, D), (D // 2) ** -0.5, 0.1875, ((0, 8), (1, 4)))
    key_weight = scatter_about(streams_of[5], (D, D), (D // 2) ** -0.5, 0.1875, ((0, 8), (1, 4)))
    value_weight = scatter_about(streams_of[6], (D, D), D ** -0.5, 0.125, ((0, 8), (1, 4)))
    query_bias = scatter_about(streams_of[7], (H, HD), 0.2, 1.25, ((0, 4), (1, 8)))
    value_bias = scatter_about(streams_of[8], (H, HD), 0.2, 1.25, ((0, 4), (1, 8)))
    output_weight = scatter_about(streams_of[9], (D, D), (D // 8) ** -0.5, 0.375, ((0, 4), (1, 8)))
    output_bias = scatter_about(streams_of[10], (D,), 0.2, 1.25, ((0, 32),), jnp.float32)
    mlp_norm_gain = jnp.clip(1.0 + 0.1 * jax.random.normal(streams_of[11], (D,), jnp.float32), 0.5, 1.5)
    mlp_norm_bias = scatter_about(streams_of[12], (D,), 0.2, 1.25, ((0, 32),), jnp.float32)
    up_weight = scatter_about(streams_of[13], (D, FF), D ** -0.5, 0.125, ((0, 8), (1, 4)))
    up_bias = scatter_about(streams_of[14], (FF // HD, HD), 0.2, 1.25, ((0, 4), (1, 8)))
    down_weight = scatter_about(streams_of[15], (FF, D), (FF // 2) ** -0.5, 0.09375, ((0, 4), (1, 8)))
    down_bias = scatter_about(streams_of[16], (D,), 0.2, 1.25, ((0, 32),), jnp.float32)
    out_grad = scatter_about(streams_of[17], (TOKENS, D), 1.0, 6.0, ((0, 32),))
    return {"hidden": hidden, "seq_lengths": seq_lengths, "attn_norm_gain": attn_norm_gain, "attn_norm_bias": attn_norm_bias, "query_weight": query_weight, "key_weight": key_weight, "value_weight": value_weight, "query_bias": query_bias, "value_bias": value_bias, "output_weight": output_weight, "output_bias": output_bias, "mlp_norm_gain": mlp_norm_gain, "mlp_norm_bias": mlp_norm_bias, "up_weight": up_weight, "up_bias": up_bias, "down_weight": down_weight, "down_bias": down_bias, "out_grad": out_grad}


EPSILON = 1e-05
GELU_COEF = math.sqrt(2.0 / math.pi)
NEGATIVE = -1e+30
HIGHEST = lax.Precision.HIGHEST

@jax.custom_vjp
def low(v):
    return lax.optimization_barrier(v.astype(jnp.bfloat16)).astype(jnp.float32)

@jax.custom_vjp
def low_back(v):
    return v

def low_keep(v):
    return (low(v), None)

def low_pass(kept, grad):
    return (grad,)

def back_keep(v):
    return (v, None)

def back_low(kept, grad):
    return (low(grad),)
low.defvjp(low_keep, low_pass)
low_back.defvjp(back_keep, back_low)

def matmul(left_mat, right_mat):
    return jnp.dot(left_mat, right_mat, precision=HIGHEST)

def layer_norm(values, norm_gain, norm_bias):
    center = values - lax.optimization_barrier(jnp.mean(values, axis=-1, keepdims=True))
    variance = lax.optimization_barrier(jnp.mean(center * center, axis=-1, keepdims=True))
    return center * lax.rsqrt(variance + EPSILON) * norm_gain + norm_bias

def gelu_tanh(values):
    return 0.5 * values * (1.0 + jnp.tanh(GELU_COEF * (values + 0.044715 * values * values * values)))

def attention(queries, keys_all, values_all, length):
    block_rows = min(512, LEN)
    block_count = LEN // block_rows
    scale = 1.0 / math.sqrt(HD)
    slopes = jnp.exp2(-8.0 * (jnp.arange(H) + 1).astype(jnp.float32) / H)
    key_pos = jnp.arange(LEN).astype(jnp.int32)

    def one_block(inputs):
        query_block, first_row = inputs
        query_pos = first_row + jnp.arange(block_rows).astype(jnp.int32)
        scores = jnp.einsum('qhd,khd->hqk', query_block, keys_all, precision=HIGHEST) * scale
        distance = (query_pos[:, None] - key_pos[None, :]).astype(jnp.float32)
        scores = low_back(scores - slopes[:, None, None] * distance)
        allowed = (key_pos[None, :] <= query_pos[:, None]) & (key_pos[None, :] < length)
        scores = jnp.where(allowed[None], scores, NEGATIVE)
        row_max = lax.optimization_barrier(jnp.max(scores, axis=-1, keepdims=True))
        exponent = jnp.exp(scores - row_max)
        attn_probs = exponent / lax.optimization_barrier(jnp.sum(exponent, axis=-1, keepdims=True))
        return jnp.einsum('hqk,khd->qhd', low(attn_probs), values_all, precision=HIGHEST)
    blocks = queries.reshape(block_count, block_rows, H, HD)
    starts = (jnp.arange(block_count) * block_rows).astype(jnp.int32)
    mixed = lax.map(jax.checkpoint(one_block), (blocks, starts))
    return mixed.reshape(LEN, D)

def layer(hidden, params, length):
    attn_norm_gain, attn_norm_bias, query_weight, key_weight, value_weight, query_bias, value_bias, output_weight, output_bias, mlp_norm_gain, mlp_norm_bias, up_weight, up_bias, down_weight, down_bias = params
    positions = jnp.arange(LEN).astype(jnp.int32)
    valid_rows = (positions < length).astype(jnp.float32)[:, None]
    normed = low(layer_norm(hidden, attn_norm_gain, attn_norm_bias))
    queries = low(low_back(matmul(normed, query_weight) + query_bias.reshape(D)))
    keys_all = low(low_back(matmul(normed, key_weight)))
    values_all = low(low_back(matmul(normed, value_weight) + value_bias.reshape(D)))
    mixed = attention(queries.reshape(LEN, H, HD), keys_all.reshape(LEN, H, HD), values_all.reshape(LEN, H, HD), length)
    mixed = low(low_back(mixed))
    middle = hidden + low_back(matmul(mixed, output_weight)) + output_bias
    second = low(layer_norm(middle, mlp_norm_gain, mlp_norm_bias))
    pre_act = low_back(matmul(second, up_weight) + up_bias.reshape(FF))
    activated = low(gelu_tanh(pre_act))
    return valid_rows * (middle + low_back(matmul(activated, down_weight)) + down_bias)

def reference(hidden, seq_lengths, attn_norm_gain, attn_norm_bias, query_weight, key_weight, value_weight, query_bias, value_bias, output_weight, output_bias, mlp_norm_gain, mlp_norm_bias, up_weight, up_bias, down_weight, down_bias, out_grad):
    params = tuple((argument.astype(jnp.float32) for argument in (attn_norm_gain, attn_norm_bias, query_weight, key_weight, value_weight, query_bias, value_bias, output_weight, output_bias, mlp_norm_gain, mlp_norm_bias, up_weight, up_bias, down_weight, down_bias)))
    sequences = hidden.astype(jnp.float32).reshape(N_DP, LEN, D)
    cotangents = out_grad.astype(jnp.float32).reshape(N_DP, LEN, D)

    def one_sequence(grad_total, inputs):
        sequence, cotangent, length = inputs

        def apply_layer(seq_in, param_in):
            return layer(seq_in, param_in, length)
        result, pullback = jax.vjp(apply_layer, sequence, params)
        seq_grad, param_grads = pullback(cotangent)
        grad_total = jax.tree.map(jnp.add, grad_total, param_grads)
        return (grad_total, (result.astype(jnp.bfloat16), seq_grad))
    zero_total = jax.tree.map(jnp.zeros_like, params)
    grad_total, (layer_out, hidden_grad) = lax.scan(one_sequence, zero_total, (sequences, cotangents, seq_lengths))
    return (layer_out.reshape(TOKENS, D), hidden_grad.reshape(TOKENS, D), grad_total[0], grad_total[1], grad_total[2], grad_total[3], grad_total[4], grad_total[5], grad_total[6], grad_total[7], grad_total[8], grad_total[9], grad_total[10], grad_total[11], grad_total[12], grad_total[13], grad_total[14])
```

```python
import functools
import math

import jax
import jax.numpy as jnp
from jax import lax
from jax.experimental import pallas as pl
from jax.experimental.pallas import tpu as pltpu
from jax.sharding import PartitionSpec as P

H = 16
HD = 128
EPSILON = 1e-05
GELU_COEF = math.sqrt(2.0 / math.pi)
NEGATIVE = -1e30
MESH = pl.DeviceIdType.MESH
F32 = jnp.float32
BF16 = jnp.bfloat16
MIB = 1024 * 1024


def norm_parts(values):
    center = values - jnp.mean(values, axis=-1, keepdims=True)
    inverse = lax.rsqrt(jnp.mean(center * center, axis=-1, keepdims=True) + EPSILON)
    return (center * inverse, inverse)


def norm_backward(upstream, unit, inverse, gain):
    scaled = upstream * gain
    return inverse * (
        scaled
        - jnp.mean(scaled, axis=-1, keepdims=True)
        - unit * jnp.mean(scaled * unit, axis=-1, keepdims=True)
    )


def gelu_pair(values):
    squared = values * values
    tanh_val = jnp.tanh(GELU_COEF * (values + 0.044715 * values * squared))
    half = 0.5 * (1.0 + tanh_val)
    slope = half + 0.5 * values * (1.0 - tanh_val * tanh_val) * GELU_COEF * (
        1.0 + 3.0 * 0.044715 * squared
    )
    return (values * half, slope)


def dot(left, right):
    return jnp.dot(left, right, preferred_element_type=F32)


def dot_rows(left, right):
    return lax.dot_general(left, right, (((0,), (0,)), ((), ())), preferred_element_type=F32)


def dot_trans(left, right):
    return lax.dot_general(left, right, (((1,), (1,)), ((), ())), preferred_element_type=F32)


def flip(index, bit):
    return index + bit - 2 * bit * ((index // bit) % 2)


def remote(src, dst, send_sem, recv_sem, device):
    return pltpu.make_async_remote_copy(
        src_ref=src,
        dst_ref=dst,
        send_sem=send_sem,
        recv_sem=recv_sem,
        device_id=device,
        device_id_type=MESH,
    )


def greet(n, plane):
    z = lax.axis_index("tensor")
    barrier = pltpu.get_barrier_semaphore()

    @pl.when(z > 0)
    def _():
        pl.semaphore_signal(barrier, inc=1, device_id={"tensor": z - 1}, device_id_type=MESH)

    @pl.when(z < n - 1)
    def _():
        pl.semaphore_signal(barrier, inc=1, device_id={"tensor": z + 1}, device_id_type=MESH)

    if plane:
        p = lax.axis_index("dp")
        for partner in (flip(p, 1), flip(p, 2), flip(p, 4), flip(flip(p, 2), 4)):
            pl.semaphore_signal(barrier, inc=1, device_id={"dp": partner}, device_id_type=MESH)

    peers = jnp.minimum(z, 1) + jnp.minimum(n - 1 - z, 1)
    pl.semaphore_wait(barrier, peers + 4 if plane else peers)


def gather_body(
    n, cut, hid, og, wq, wk, wv, wo, up, down,
    hid_all, og_all, wqkv_all, wo_all, up_all, down_all,
    zsend, zrecv, wsend, wrecv, lsem,
):
    z = lax.axis_index("tensor")
    p = lax.axis_index("dp")
    piece = hid.shape[0] // cut
    shards = (wq, wk, wv, wo, up, down)
    part, width = wq.shape
    evens = {2: flip(p, 2), 4: flip(p, 4), 6: flip(flip(p, 2), 4)}
    sibling = flip(p, 1)
    zin = (hid, og)
    zout = (hid_all, og_all)

    def slot(i, q):
        if i < 3:
            return wqkv_all.at[pl.ds(q * part, part), pl.ds(i * width, width)]
        if i == 3:
            return wo_all.at[:, pl.ds(q * part, part)]
        if i == 4:
            return up_all.at[pl.ds(q * part, part), :]
        return down_all.at[:, pl.ds(q * part, part)]

    def direct(i, q):
        return remote(shards[i], slot(i, p), wsend.at[i, q], wrecv.at[i, q], {"dp": evens[q]})

    def relay(i, q):
        owner = p if q == 0 else evens[q]
        src = shards[i] if q == 0 else slot(i, owner)
        return remote(src, slot(i, owner), wsend.at[i, q + 1], wrecv.at[i, q + 1], {"dp": sibling})

    def zcopy(a, way, k, c, shard):
        to = z + 1 if way == 0 else z - 1
        rows = pl.ds(c * piece, piece)
        src = zin[a].at[rows, :] if k == 0 else zout[a].at[shard, rows, :]
        dst = zout[a].at[shard, rows, :]
        return remote(src, dst, zsend.at[a, way, k, c], zrecv.at[a, way, k, c], {"tensor": to})

    def zsend_hop(a, k, c):
        @pl.when(jnp.logical_and(z >= k, z <= n - 2))
        def _():
            zcopy(a, 0, k, c, z - k).start()

        @pl.when(jnp.logical_and(z + k <= n - 1, z >= 1))
        def _():
            zcopy(a, 1, k, c, z + k).start()

    def zstep(a, k):
        for c in range(cut):
            @pl.when(z >= k)
            def _():
                zcopy(a, 0, k - 1, c, z - k).wait_recv()

            @pl.when(z + k <= n - 1)
            def _():
                zcopy(a, 1, k - 1, c, z + k).wait_recv()

            if k < n - 1:
                zsend_hop(a, k, c)

    def zdrain(a):
        for k in range(n - 1):
            for c in range(cut):
                @pl.when(jnp.logical_and(z >= k, z <= n - 2))
                def _():
                    zcopy(a, 0, k, c, z - k).wait_send()

                @pl.when(jnp.logical_and(z + k <= n - 1, z >= 1))
                def _():
                    zcopy(a, 1, k, c, z + k).wait_send()

    def forward(i):
        for q in (2, 4, 6):
            direct(i, q).wait_recv()
            relay(i, q).start()

    greet(n, True)
    for c in range(cut):
        zsend_hop(0, 0, c)
    for i in range(6):
        for q in (2, 4, 6):
            direct(i, q).start()
        relay(i, 0).start()
    for c in range(cut):
        zsend_hop(1, 0, c)
    local = [pltpu.make_async_copy(zin[a], zout[a].at[z], lsem.at[a]) for a in range(2)]
    local += [pltpu.make_async_copy(shards[i], slot(i, p), lsem.at[2 + i]) for i in range(6)]
    for copy in local:
        copy.start()
    zstep(0, 1)
    forward(0)
    forward(1)
    forward(2)
    for k in range(2, n):
        zstep(0, k)
        zstep(1, k - 1)
    forward(3)
    forward(4)
    zstep(1, n - 1)
    forward(5)
    for i in range(6):
        for q in (0, 2, 4, 6):
            relay(i, q).wait_recv()
    for i in range(6):
        for q in (2, 4, 6):
            direct(i, q).wait_send()
        for q in (0, 2, 4, 6):
            relay(i, q).wait_send()
    zdrain(0)
    zdrain(1)
    for copy in local:
        copy.wait()


def gather_inputs(n, hid, og, weights, cut=2):
    wq, _, _, wo, up, down = weights
    rows, d = hid.shape
    dp = lax.axis_size("dp")
    if dp != 8:
        along = lambda w, axis: lax.all_gather(w, "dp", axis=axis, tiled=True)
        wqkv = jnp.concatenate(weights[:3], axis=1)
        return (
            lax.all_gather(hid, "tensor"),
            lax.all_gather(og, "tensor"),
            along(wqkv, 0),
            along(wo, 1),
            along(up, 0),
            along(down, 1),
        )
    out = lambda *shape: jax.ShapeDtypeStruct(shape, BF16)
    return pl.pallas_call(
        functools.partial(gather_body, n, cut),
        out_shape=(
            out(n, rows, d),
            out(n, rows, d),
            out(wq.shape[0] * dp, 3 * wq.shape[1]),
            out(wo.shape[0], wo.shape[1] * dp),
            out(up.shape[0] * dp, up.shape[1]),
            out(down.shape[0], down.shape[1] * dp),
        ),
        in_specs=[pl.BlockSpec(memory_space=pltpu.VMEM)] * 8,
        out_specs=[pl.BlockSpec(memory_space=pl.ANY)] * 6,
        scratch_shapes=[
            pltpu.SemaphoreType.DMA((2, 2, n - 1, cut)),
            pltpu.SemaphoreType.DMA((2, 2, n - 1, cut)),
            pltpu.SemaphoreType.DMA((6, 8)),
            pltpu.SemaphoreType.DMA((6, 8)),
            pltpu.SemaphoreType.DMA((8,)),
        ],
        compiler_params=pltpu.CompilerParams(
            collective_id=0, has_side_effects=True, vmem_limit_bytes=16 * MIB
        ),
        name="gather_inputs",
    )(hid, og, *weights)


def block_scores(query_block, keys_all, first_row, slopes, seq_len):
    block_rows = query_block.shape[0]
    key_rows = keys_all.shape[0]
    scale = 1.0 / math.sqrt(HD)
    scores = jnp.einsum("qhd,khd->hqk", query_block, keys_all, preferred_element_type=F32) * scale
    query_pos = first_row + lax.iota(jnp.int32, block_rows)
    key_pos = lax.iota(jnp.int32, key_rows)
    distance = (query_pos[:, None] - key_pos[None, :]).astype(F32)
    scores = scores - slopes[:, None, None] * distance
    allowed = (key_pos[None, :] <= query_pos[:, None]) & (key_pos[None, :] < seq_len)
    return jnp.where(allowed[None], scores, NEGATIVE)


def attend_forward(queries, keys_all, values_all, slopes, seq_len):
    key_rows, head_count, head_dim = queries.shape
    block_rows = min(512, key_rows)
    block_count = key_rows // block_rows
    blocks = queries.reshape(block_count, block_rows, head_count, head_dim)
    starts = lax.iota(jnp.int32, block_count) * block_rows

    def one_block(inputs):
        query_block, first_row = inputs
        scores = block_scores(query_block, keys_all, first_row, slopes, seq_len)
        row_max = jnp.max(scores, axis=-1, keepdims=True)
        log_total = row_max + jnp.log(jnp.sum(jnp.exp(scores - row_max), axis=-1, keepdims=True))
        attn_probs = jnp.exp(scores - log_total).astype(BF16)
        block_out = jnp.einsum("hqk,khd->qhd", attn_probs, values_all, preferred_element_type=F32)
        return (block_out, log_total[..., 0])

    mixed, log_sums = lax.map(one_block, (blocks, starts))
    return (mixed.reshape(key_rows, head_count * head_dim), log_sums)


def attend_backward(queries, keys_all, values_all, mixed_grad, log_sums, slopes, seq_len):
    key_rows, head_count, head_dim = queries.shape
    block_rows = min(512, key_rows)
    block_count = key_rows // block_rows
    scale = 1.0 / math.sqrt(head_dim)
    blocks = queries.reshape(block_count, block_rows, head_count, head_dim)
    grad_blocks = mixed_grad.reshape(block_count, block_rows, head_count, head_dim)
    starts = lax.iota(jnp.int32, block_count) * block_rows

    def one_block(carried, inputs):
        key_acc, value_acc = carried
        query_block, grad_block, sum_block, first_row = inputs
        scores = block_scores(query_block, keys_all, first_row, slopes, seq_len)
        attn_probs = jnp.exp(scores - sum_block[..., None])
        prob_grad = jnp.einsum("qhd,khd->hqk", grad_block, values_all, preferred_element_type=F32)
        value_acc = value_acc + jnp.einsum(
            "hqk,qhd->khd", attn_probs.astype(BF16), grad_block, preferred_element_type=F32
        )
        row_delta = jnp.sum(attn_probs * prob_grad, axis=-1, keepdims=True)
        score_grad = (attn_probs * (prob_grad - row_delta)).astype(BF16)
        query_grad = (
            jnp.einsum("hqk,khd->qhd", score_grad, keys_all, preferred_element_type=F32) * scale
        )
        key_acc = (
            key_acc
            + jnp.einsum("hqk,qhd->khd", score_grad, query_block, preferred_element_type=F32)
            * scale
        )
        return ((key_acc, value_acc), query_grad)

    zero_acc = jnp.zeros((key_rows, head_count, head_dim), F32)
    (key_grad, value_grad), query_grad = lax.scan(
        one_block, (zero_acc, zero_acc), (blocks, grad_blocks, log_sums, starts)
    )
    flat = (key_rows, head_count * head_dim)
    return (query_grad.reshape(flat), key_grad.reshape(flat), value_grad.reshape(flat))


def scatter_rows(partial_sum):
    return lax.psum_scatter(
        partial_sum.astype(BF16), "tensor", scatter_dimension=0, tiled=True
    ).astype(F32)


def gather_rows(rows):
    return lax.all_gather(rows.astype(BF16), "tensor", axis=0, tiled=True)


def middle_part(n, mixed, wo, up, down, up_add, out_bias, gain_two, bias_two, hidden_f, upstream, og_low):
    middle = hidden_f + scatter_rows(dot(mixed, wo)) + out_bias
    unit_two, inverse_two = norm_parts(middle)
    mlp_input = gather_rows(unit_two * gain_two + bias_two)
    act_value, act_slope = gelu_pair(dot(mlp_input, up) + up_add)
    activated = act_value.astype(BF16)
    mlp_partial = dot(activated, down).astype(BF16)
    pre_grad = (dot_trans(og_low, down) * act_slope).astype(BF16)
    second_grad = scatter_rows(dot_trans(pre_grad, up))
    middle_grad = upstream + norm_backward(second_grad, unit_two, inverse_two, gain_two)
    grad_attn = gather_rows(middle_grad)
    mixed_grad = dot_trans(grad_attn, wo).astype(BF16)
    sums = (jnp.sum(second_grad * unit_two, axis=0), jnp.sum(second_grad, axis=0))
    return (middle, mlp_input, activated, mlp_partial, pre_grad, middle_grad, grad_attn, mixed_grad, sums)


def shards(
    hidden, seq_lengths, attn_norm_gain, attn_norm_bias, query_weight, key_weight, value_weight,
    query_bias, value_bias, output_weight, output_bias, mlp_norm_gain, mlp_norm_bias, up_weight,
    up_bias, down_weight, down_bias, out_grad,
):
    n = lax.axis_size("tensor")
    dp = lax.axis_size("dp")
    z = lax.axis_index("tensor")
    rows, d = hidden.shape
    heads, hd_part = query_bias.shape
    up_heads = up_bias.shape[0]
    width = query_weight.shape[1]
    seq_len = seq_lengths[0]
    valid = (z * rows + lax.iota(jnp.int32, rows) < seq_len).astype(F32)[:, None]

    vec = attn_norm_gain.shape[0]
    heads_all = 2 * heads + up_heads
    packed = jnp.concatenate(
        [
            jnp.stack(
                [attn_norm_gain, attn_norm_bias, output_bias, mlp_norm_gain, mlp_norm_bias, down_bias]
            ).reshape(-1),
            jnp.concatenate([query_bias, value_bias, up_bias]).astype(F32).reshape(-1),
        ]
    )
    packed = lax.all_gather(packed, ("dp", "tensor"), axis=0)
    vectors = packed[:, : 6 * vec].reshape(dp * n, 6, vec).transpose(1, 0, 2).reshape(6, d)
    gain_one, bias_one, out_bias, gain_two, bias_two, last_bias = (vectors[i] for i in range(6))
    biases = lax.dynamic_index_in_dim(
        packed[:, 6 * vec :].reshape(dp, n, heads_all, hd_part), z, 1, keepdims=False
    )
    biases = biases.transpose(1, 0, 2).reshape(heads_all * HD)
    query_add, value_add, up_add = (
        biases[:width],
        biases[width : 2 * width],
        biases[2 * width :],
    )

    upstream = out_grad.astype(F32) * valid
    hid_all, og_all, wqkv, wo, up, down = gather_inputs(
        n,
        hidden,
        upstream.astype(BF16),
        (query_weight, key_weight, value_weight, output_weight, up_weight, down_weight),
    )
    key_rows = n * rows
    og_low = og_all.reshape(key_rows, d)
    head_ids = (z * heads + lax.iota(jnp.int32, heads) + 1).astype(F32)
    slopes = jnp.exp2(head_ids * (-8.0 / H))

    unit_all, _ = norm_parts(hid_all.reshape(key_rows, d).astype(F32))
    attn_input = (unit_all * gain_one + bias_one).astype(BF16)
    qkv_add = jnp.concatenate([query_add, jnp.zeros_like(query_add), value_add])
    qkv = (dot(attn_input, wqkv) + qkv_add).astype(BF16)
    queries, keys_all, values_all = (
        qkv[:, i * width : (i + 1) * width].reshape(key_rows, heads, HD) for i in range(3)
    )
    mixed_f, log_sums = attend_forward(queries, keys_all, values_all, slopes, seq_len)
    mixed = mixed_f.astype(BF16)

    hidden_f = hidden.astype(F32)
    middle, mlp_input, activated, mlp_partial, pre_grad, middle_grad, grad_attn, mixed_grad, sums = (
        middle_part(
            n, mixed, wo, up, down, up_add, out_bias, gain_two, bias_two, hidden_f, upstream, og_low
        )
    )
    gain_two_grad, bias_two_grad = sums
    mlp_branch = lax.psum_scatter(mlp_partial, "tensor", scatter_dimension=0, tiled=True)
    layer_out = (valid * (middle + mlp_branch.astype(F32) + last_bias)).astype(BF16)

    down_grad = dot_rows(activated, og_low)
    up_grad = dot_rows(mlp_input, pre_grad)
    up_add_grad = jnp.sum(pre_grad.astype(F32), axis=0)
    out_grad_mat = dot_rows(mixed, grad_attn)

    query_grad, key_grad, value_grad = attend_backward(
        queries, keys_all, values_all, mixed_grad.reshape(queries.shape), log_sums, slopes, seq_len
    )
    qkv_grad = jnp.concatenate([query_grad, key_grad, value_grad], axis=1).astype(BF16)
    qkv_mat_grad = dot_rows(attn_input, qkv_grad)
    qkv_add_grad = jnp.sum(qkv_grad.astype(F32), axis=0)
    first_grad = scatter_rows(dot_trans(qkv_grad, wqkv))
    unit_one, inverse_one = norm_parts(hidden_f)
    hidden_grad = middle_grad + norm_backward(first_grad, unit_one, inverse_one, gain_one)

    over_dp = lambda w, axis: lax.psum_scatter(
        w.astype(BF16), "dp", scatter_dimension=axis, tiled=True
    ).astype(F32)
    qkv_out = over_dp(qkv_mat_grad, 0)
    query_out, key_out, value_out = (qkv_out[:, i * width : (i + 1) * width] for i in range(3))
    wo_out = over_dp(out_grad_mat, 1)
    up_out = over_dp(up_grad, 0)
    down_out = over_dp(down_grad, 1)
    vec_grads = jnp.stack(
        [
            jnp.sum(first_grad * unit_one, axis=0),
            jnp.sum(first_grad, axis=0),
            jnp.sum(middle_grad, axis=0),
            gain_two_grad,
            bias_two_grad,
            jnp.sum(upstream, axis=0),
        ]
    )
    vec_grads = vec_grads.reshape(6, dp * n, vec).transpose(1, 0, 2).reshape(dp, n, 6 * vec)
    bias_grads = jnp.concatenate([qkv_add_grad[:width], qkv_add_grad[2 * width :], up_add_grad])
    bias_grads = bias_grads.reshape(heads_all, dp, hd_part).transpose(1, 0, 2).reshape(dp, 1, -1)
    mine = (lax.iota(jnp.int32, n) == z).astype(F32)[None, :, None]
    small = jnp.concatenate([vec_grads, bias_grads * mine], axis=2).reshape(dp * n, -1)
    small = lax.psum_scatter(small, ("dp", "tensor"), scatter_dimension=0, tiled=True)[0]
    vec_out = small[: 6 * vec].reshape(6, vec)
    bias_out = small[6 * vec :].reshape(heads_all, hd_part)
    return (
        layer_out,
        hidden_grad,
        vec_out[0],
        vec_out[1],
        query_out,
        key_out,
        value_out,
        bias_out[:heads],
        bias_out[heads : 2 * heads],
        wo_out,
        vec_out[2],
        vec_out[3],
        vec_out[4],
        up_out,
        bias_out[2 * heads :],
        down_out,
        vec_out[5],
    )


def solution(mesh):
    vector = P(("dp", "tensor"))
    rows = P(("dp", "tensor"), None)
    wide = P("dp", "tensor")
    tall = P("tensor", "dp")
    return jax.shard_map(
        shards,
        mesh=mesh,
        in_specs=(
            rows, P("dp"), vector, vector, wide, wide, wide, tall, tall, tall, vector, vector,
            vector, wide, tall, tall, vector, rows,
        ),
        out_specs=(
            rows, rows, vector, vector, wide, wide, wide, tall, tall, tall, vector, vector,
            vector, wide, tall, tall, vector,
        ),
        check_vma=False,
    )
```
